32 devices in a mesh: pipe: 4 (over y, x), dp: 4 (over z), tensor: 2 (over core).
Axes of the slice: x: 2, y: 2, z: 4, core: 2. Of those that a mesh axis runs over, the one named last changes fastest.
Arguments:
- llm_grad: bfloat16 [4, 128, 1664], P(None, 'dp'), may hold values from -6 to 6
- slot_row: int32 [4, 4, 32], P(None, 'dp'), may hold values from 0 to 31, each once within a row
- counts: int32 [4, 4], P('dp'), may hold values from 8 to 32, as said below
- saved_in: bfloat16 [4, 4, 128, 1664], P('pipe', None, 'dp'), may hold values from -6 to 6
- saved_pre: bfloat16 [4, 4, 128, 6400], P('pipe', None, 'dp', 'tensor'), may hold values from -6 to 6
- weights: bfloat16 [4, 1664, 6400], P('pipe', 'dp', 'tensor'), may hold values from -0.15625 to 0.15625
- channel_scale: float32 [4, 1664], P('pipe'), may hold values from 0.25 to 2
Outputs:
- weight_grad: bfloat16 [4, 1664, 6400], P('pipe', 'dp', 'tensor')
- section_grad: bfloat16 [4, 4, 128, 1664], P('pipe', None, 'dp')
The draws below stay inside these ranges and needn't reach their ends.
Inputs may be any that keep to these rules, and one draw needn't show every extreme that they name: For each micro-batch and rank, slot_row lists every row of the rank once. `counts`: both ends of the range occur in every draw.
All inputs are finite; a program needn't handle non-finite values.
Results may differ from the reference program's by a relative error of at most 0.023.
Values may be sent and summed in bfloat16 or wider, within the bound.
No kernel may reach another device: no remote copies, remote signals or barrier semaphores. Data moves between devices by JAX's collectives and lax.ppermute only.
A program may use at most 128 MiB of HBM per device.

```python
import math
import jax
import jax.numpy as jnp
from jax import lax

D = 1664
FF = 6400
ROWS = 32
MICRO = 4
SECTIONS = 4
RANKS = 4
TOKENS = 128


def draw_counts(key, part):
    key_values, key_high, key_low = jax.random.split(key, 3)
    count_all = RANKS * MICRO
    values = jax.random.randint(key_values, (count_all,), ROWS // 4, ROWS + 1, dtype=jnp.int32)
    high_at = jax.random.randint(key_high, (), 0, count_all, dtype=jnp.int32)
    low_at = (high_at + 1 + jax.random.randint(key_low, (), 0, count_all - 1, dtype=jnp.int32)) % count_all
    places = jnp.arange(count_all, dtype=jnp.int32)
    values = jnp.where(places == high_at, ROWS, values)
    values = jnp.where(places == low_at, ROWS // 4, values)
    return values.reshape(RANKS, MICRO).astype(jnp.int32)


def steps_of(own_key, dims, cuts, smallest, largest):
    factor_of, own = 1.0, jax.random.fold_in(own_key, 6)
    for axis_at, parts in cuts:
        heights = jnp.exp(jax.random.uniform(jax.random.fold_in(own, axis_at), (parts,), jnp.float32, smallest / len(cuts), largest / len(cuts)))
        factor_of = factor_of * jnp.repeat(heights, dims[axis_at] // parts).reshape([-1 if axis == axis_at else 1 for axis in range(len(dims))])
    return factor_of


def centred(rng, extent, scale, reach, pieces=(), held_as=jnp.bfloat16):
    drawn = jax.random.normal(rng, extent, jnp.float32) * scale
    if len(pieces) > 0:
        drawn = steps_of(rng, extent, pieces, -0.22, 0.18) * drawn
    return jnp.clip(drawn, min=-reach, max=reach).astype(held_as)


def setup_inputs(seed: int = 0) -> dict:
    keys = jax.random.split(jax.random.key(seed), 8)
    return {
        "llm_grad": centred(keys[0], (MICRO, TOKENS, D), 1.0, 6.0, ((1, 4),)),
        "slot_row": jax.vmap(lambda own: jax.random.permutation(own, ROWS))(jax.random.split(keys[1], MICRO * RANKS)).reshape((MICRO, RANKS, ROWS)).astype(jnp.int32),
        "counts": draw_counts(jax.random.fold_in(keys[7], 71), 0),
        "saved_in": centred(keys[3], (SECTIONS, MICRO, TOKENS, D), 1.0, 6.0, ((0, 4), (2, 4))),
        "saved_pre": centred(keys[4], (SECTIONS, MICRO, TOKENS, FF), 1.0, 6.0, ((0, 4), (2, 4), (3, 2))),
        "weights": centred(keys[5], (SECTIONS, D, FF), D ** -0.5, 0.15625, ((0, 4), (1, 4), (2, 2))),
        "channel_scale": jnp.clip(jnp.exp(math.log(2.0) - 2.0794415 * jax.random.uniform(keys[6], (SECTIONS, D), jnp.float32) ** steps_of(keys[6], (SECTIONS, D), ((0, 4),), -0.2, 0.2)), 0.25, 2.0),
    }


norm_eps = 1e-06
root_half = 0.7071067811865476
inv_root_two_pi = 0.3989422804014327

def gelu_parts(pre_act):
    normal_cdf = 0.5 * (1.0 + jax.scipy.special.erf(pre_act * root_half))
    density = jnp.exp(-0.5 * pre_act * pre_act) * inv_root_two_pi
    return (pre_act * normal_cdf, normal_cdf + pre_act * density)

def top_gradient(llm_grad, slot_row, counts):
    slot_ids = jnp.arange(ROWS, dtype=jnp.int32)
    kept_mask = slot_ids[None, None, :] < jnp.transpose(counts)[:, :, None]
    source = llm_grad.reshape(MICRO, RANKS, ROWS, D).astype(jnp.float32)
    source = jnp.where(kept_mask[..., None], source, jnp.zeros_like(source))
    onehot = (slot_row[..., :, None] == slot_ids[None, None, None, :]).astype(jnp.float32)
    placed = jnp.einsum('abjr,abjd->abrd', onehot, source)
    return placed.reshape(MICRO, TOKENS, D).astype(jnp.bfloat16)

def rank_sum(left_side, right_side):
    left_ranks = left_side.reshape(MICRO, RANKS, ROWS, D)
    right_ranks = right_side.reshape(MICRO, RANKS, ROWS, FF)

    def add_rank(grad_total, rank_index):
        left_part = lax.dynamic_index_in_dim(left_ranks, rank_index, 1, keepdims=False).reshape(MICRO * ROWS, D)
        right_part = lax.dynamic_index_in_dim(right_ranks, rank_index, 1, keepdims=False).reshape(MICRO * ROWS, FF)
        term = jnp.dot(left_part.T, right_part, preferred_element_type=jnp.float32)
        rounded = lax.optimization_barrier(term.astype(jnp.bfloat16))
        return (grad_total + rounded.astype(jnp.float32), None)
    grad_total, unused = lax.scan(add_rank, jnp.zeros((D, FF), jnp.float32), jnp.arange(RANKS, dtype=jnp.int32))
    return grad_total.astype(jnp.bfloat16)

def reference(llm_grad, slot_row, counts, saved_in, saved_pre, weights, channel_scale):
    incoming = top_gradient(llm_grad, slot_row, counts)
    hidden_grad = None
    section_list = []
    weight_list = []
    for section_index in range(SECTIONS - 1, -1, -1):
        channel_gain = channel_scale[section_index]
        weight_now = weights[section_index]
        pre_act = saved_pre[section_index].astype(jnp.float32)
        if section_index % 2 == 1:
            scaled = (incoming.astype(jnp.float32) * channel_gain).astype(jnp.bfloat16)
            hidden_grad = jnp.dot(scaled.reshape(-1, D), weight_now, preferred_element_type=jnp.float32)
            hidden_grad = hidden_grad.reshape(MICRO, TOKENS, FF).astype(jnp.bfloat16)
            activated = gelu_parts(pre_act)[0].astype(jnp.bfloat16)
            outgoing = incoming
            left_side, right_side = (scaled, activated)
        else:
            act_grad = (hidden_grad.astype(jnp.float32) * gelu_parts(pre_act)[1]).astype(jnp.bfloat16)
            values = saved_in[section_index].astype(jnp.float32)
            center = values - lax.optimization_barrier(jnp.mean(values, axis=-1, keepdims=True))
            inv_std = lax.rsqrt(lax.optimization_barrier(jnp.mean(center * center, axis=-1, keepdims=True)) + norm_eps)
            unit_rows = center * inv_std
            normed = (unit_rows * channel_gain).astype(jnp.bfloat16)
            dnorm = jnp.dot(act_grad.reshape(-1, FF), weight_now.T, preferred_element_type=jnp.float32)
            scaled_back = dnorm.reshape(MICRO, TOKENS, D) * channel_gain
            back = inv_std * (scaled_back - lax.optimization_barrier(jnp.mean(scaled_back, axis=-1, keepdims=True)) - unit_rows * lax.optimization_barrier(jnp.mean(scaled_back * unit_rows, axis=-1, keepdims=True)))
            outgoing = (incoming.astype(jnp.float32) + back).astype(jnp.bfloat16)
            left_side, right_side = (normed, act_grad)
        section_list.append(outgoing)
        weight_list.append(rank_sum(left_side, right_side))
        incoming = outgoing
    section_grad = jnp.stack(section_list[::-1], axis=0)
    weight_grad = jnp.stack(weight_list[::-1], axis=0)
    return (weight_grad, section_grad)
```

```python
import jax
import jax.numpy as jnp
from jax import lax
from jax.sharding import PartitionSpec as P

norm_eps = 1e-06
root_half = 0.7071067811865476
inv_root_two_pi = 0.3989422804014327
lanes = 128


def gelu_parts(pre_act):
    normal_cdf = 0.5 * (1.0 + jax.scipy.special.erf(pre_act * root_half))
    density = jnp.exp(-0.5 * pre_act * pre_act) * inv_root_two_pi
    return (pre_act * normal_cdf, normal_cdf + pre_act * density)


def local_top(llm_grad, slot_row, counts):
    row_count = llm_grad.shape[1]
    slot_ids = jnp.arange(row_count, dtype=jnp.int32)
    kept_mask = slot_ids[None, :] < counts[:, None]
    source = jnp.where(kept_mask[..., None], llm_grad, jnp.zeros_like(llm_grad))
    onehot = (slot_row[:, :, None] == slot_ids[None, None, :]).astype(jnp.bfloat16)
    placed = jnp.einsum("mjr,mjd->mrd", onehot, source, preferred_element_type=jnp.float32)
    return placed.astype(jnp.bfloat16)


def cuts(hidden, parts):
    unit = lanes if hidden % lanes == 0 else 1
    tiles = hidden // unit
    bounds = [tiles * i // parts * unit for i in range(parts + 1)]
    width = max(b - a for a, b in zip(bounds, bounds[1:]))
    return bounds, width


def split_hidden(block, parts):
    bounds, width = cuts(block.shape[-1], parts)
    lead = [(0, 0)] * (block.ndim - 1)
    return jnp.stack(
        [
            jnp.pad(block[..., a:b], lead + [(0, width - (b - a))])
            for a, b in zip(bounds, bounds[1:])
        ]
    )


def merge_hidden(blocks, hidden):
    bounds, width = cuts(hidden, blocks.shape[0])
    return jnp.concatenate(
        [blocks[i][..., : b - a] for i, (a, b) in enumerate(zip(bounds, bounds[1:]))], axis=-1
    )


def exchange(blocks, axes):
    return lax.all_to_all(blocks, axes, 0, 0, tiled=True)


def swap_cores(block):
    return lax.ppermute(block, "tensor", [(0, 1), (1, 0)])


def dot32(left, right, dims):
    return lax.dot_general(left, right, (dims, ((), ())), preferred_element_type=jnp.float32)


def body(llm_grad, slot_row, counts, saved_in, saved_pre, weights, channel_scale):
    sections = lax.axis_size("pipe")
    ranks = lax.axis_size("dp")
    core = lax.axis_index("tensor")
    micro_count, row_count, model_width = llm_grad.shape
    hidden = saved_pre.shape[3]
    tokens = micro_count * row_count
    channels = weights.shape[1]
    columns = sections
    part = tokens // (2 * columns)
    channel_gain = channel_scale[0]

    def all_ranks_rows(rows):
        kinds = rows.shape[0]
        sliced = rows.reshape(kinds, part, ranks, channels).transpose(2, 0, 1, 3)
        sent = jnp.broadcast_to(sliced[:, None], (ranks, columns, kinds, part, channels))
        got = exchange(sent.reshape(ranks * columns, kinds, part, channels), ("dp", "pipe"))
        other = swap_cores(got)
        first = jnp.where(core == 0, got, other)
        second = jnp.where(core == 0, other, got)
        both = jnp.stack([first, second], axis=1)
        return both.transpose(2, 0, 1, 3, 4).reshape(kinds, ranks * tokens, channels)

    def sum_to_rows(partial_sum):
        halves = partial_sum.reshape(ranks * columns, 2, part, channels)
        keep = jnp.where(core == 0, halves[:, 0], halves[:, 1])
        give = jnp.where(core == 0, halves[:, 1], halves[:, 0]).astype(jnp.bfloat16)
        pair = (keep + swap_cores(give).astype(jnp.float32)).astype(jnp.bfloat16)
        got = exchange(pair, ("dp", "pipe")).reshape(ranks, columns, part, channels)
        summed = jnp.sum(got.astype(jnp.float32), axis=1)
        return summed.transpose(1, 0, 2).reshape(part, model_width)

    def sum_over_ranks(partial_sum):
        sent = partial_sum.astype(jnp.bfloat16).reshape(ranks, tokens, -1)
        return jnp.sum(exchange(sent, "dp").astype(jnp.float32), axis=0)

    def all_ranks(block):
        kinds = block.shape[0]
        sent = jnp.broadcast_to(block[None], (ranks,) + block.shape)
        got = exchange(sent, "dp")
        return got.transpose(1, 0, 2, 3).reshape(kinds, ranks * tokens, -1)

    top_grad = local_top(llm_grad, slot_row[:, 0], counts[0])
    top_flat = top_grad.reshape(tokens, model_width)
    scaled_weight = (weights[0].astype(jnp.float32) * channel_gain_rows(channel_gain, channels)).astype(
        jnp.bfloat16
    )
    weight_parts = exchange(split_hidden(scaled_weight, columns), "pipe")
    top_sliced = top_flat.reshape(tokens, ranks, channels).transpose(1, 0, 2)
    grad_all = exchange(top_sliced, "dp").reshape(ranks * tokens, channels)
    pre_parts = exchange(split_hidden(saved_pre[0].reshape(tokens, hidden), columns), "pipe")
    in_halves = saved_in[0].reshape(columns, 2, part, model_width)
    in_half = jnp.where(core == 0, in_halves[:, 0], in_halves[:, 1])
    in_parts = exchange(in_half, "pipe")

    def gain_free_norm(values):
        values = values.astype(jnp.float32)
        center = values - jnp.mean(values, axis=-1, keepdims=True)
        inv_std = lax.rsqrt(jnp.mean(center * center, axis=-1, keepdims=True) + norm_eps)
        return center * inv_std, inv_std

    ups = list(range(sections - 2, -1, -2))
    downs = list(range(sections - 1, -1, -2))
    units = {}
    for s in ups:
        units[s] = gain_free_norm(in_parts[s])
    unit_all = all_ranks_rows(jnp.stack([units[s][0].astype(jnp.bfloat16) for s in ups]))
    activated = jnp.stack(
        [gelu_parts(pre_parts[s].astype(jnp.float32))[0].astype(jnp.bfloat16) for s in downs]
    )
    activated_all = all_ranks(activated)

    top_halves = top_flat.reshape(columns, 2, part, model_width)
    column = lax.axis_index("pipe")
    own = lax.dynamic_index_in_dim(top_halves, column, 0, keepdims=False)
    incoming = jnp.where(core == 0, own[0], own[1])
    weight_grads = [None] * sections
    outgoing = [None] * sections
    for pair, (up, down) in enumerate(zip(ups, downs)):
        partial_hidden = dot32(grad_all, weight_parts[down], ((1,), (0,)))
        hidden_grad = sum_over_ranks(partial_hidden)
        slope = gelu_parts(pre_parts[up].astype(jnp.float32))[1]
        act_grad = all_ranks((hidden_grad * slope).astype(jnp.bfloat16)[None])[0]
        back = sum_to_rows(dot32(act_grad, weight_parts[up], ((1,), (1,))))
        unit, inv_std = units[up]
        back = inv_std * (
            back
            - jnp.mean(back, axis=-1, keepdims=True)
            - unit * jnp.mean(back * unit, axis=-1, keepdims=True)
        )
        weight_grads[down] = dot32(grad_all, activated_all[pair], ((0,), (0,)))
        weight_grads[up] = dot32(unit_all[pair], act_grad, ((0,), (0,)))
        outgoing[down] = incoming
        incoming = (incoming.astype(jnp.float32) + back).astype(jnp.bfloat16)
        outgoing[up] = incoming
        if up > 0:
            grad_all = all_ranks_rows(incoming[None])[0]

    returned = exchange(jnp.stack(weight_grads).astype(jnp.bfloat16), "pipe")
    merged = merge_hidden(returned, hidden).astype(jnp.float32)
    weight_out = (merged * channel_gain_rows(channel_gain, channels)).astype(jnp.bfloat16)

    sent_rows = exchange(jnp.stack(outgoing), "pipe")
    other_rows = swap_cores(sent_rows)
    first = jnp.where(core == 0, sent_rows, other_rows)
    second = jnp.where(core == 0, other_rows, sent_rows)
    section_out = jnp.stack([first, second], axis=1).reshape(micro_count, row_count, model_width)
    return (weight_out[None], section_out[None])


def channel_gain_rows(channel_gain, channels):
    start = lax.axis_index("dp") * channels
    return lax.dynamic_slice_in_dim(channel_gain, start, channels, 0)[:, None]


def solution(mesh):
    in_specs = (
        P(None, "dp", None),
        P(None, "dp", None),
        P("dp", None),
        P("pipe", None, "dp", None),
        P("pipe", None, "dp", "tensor"),
        P("pipe", "dp", "tensor"),
        P("pipe", None),
    )
    out_specs = (P("pipe", "dp", "tensor"), P("pipe", None, "dp", None))
    return jax.shard_map(body, mesh=mesh, in_specs=in_specs, out_specs=out_specs, check_vma=False)
```

```python
import jax
import jax.numpy as jnp
from jax import lax
from jax.sharding import PartitionSpec as P

norm_eps = 1e-06
root_half = 0.7071067811865476
inv_root_two_pi = 0.3989422804014327
lanes = 128
aside_limit = 8


def gelu_parts(pre_act):
    normal_cdf = 0.5 * (1.0 + jax.scipy.special.erf(pre_act * root_half))
    density = jnp.exp(-0.5 * pre_act * pre_act) * inv_root_two_pi
    return (pre_act * normal_cdf, normal_cdf + pre_act * density)


def local_top(llm_grad, slot_row, counts):
    row_count = llm_grad.shape[1]
    slot_ids = jnp.arange(row_count, dtype=jnp.int32)
    kept_mask = slot_ids[None, :] < counts[:, None]
    source = jnp.where(kept_mask[..., None], llm_grad, jnp.zeros_like(llm_grad))
    onehot = (slot_row[:, :, None] == slot_ids[None, None, :]).astype(jnp.bfloat16)
    placed = jnp.einsum("mjr,mjd->mrd", onehot, source, preferred_element_type=jnp.float32)
    return placed.astype(jnp.bfloat16)


def cuts(hidden, parts):
    unit = lanes if hidden % lanes == 0 else 1
    tiles = hidden // unit
    bounds = [tiles * i // parts * unit for i in range(parts + 1)]
    width = max(b - a for a, b in zip(bounds, bounds[1:]))
    starts = [min(a, hidden - width) for a in bounds[:-1]]
    fresh = [b - a for a, b in zip(starts, starts[1:] + [hidden])]
    return starts, fresh, width


def lookup(values, index):
    found = jnp.int32(values[-1])
    for i, value in enumerate(values[:-1]):
        found = jnp.where(index == i, jnp.int32(value), found)
    return found


def exchange(blocks, axes):
    return lax.all_to_all(blocks, axes, 0, 0, tiled=True)


def swap_cores(block):
    return lax.ppermute(block, "tensor", [(0, 1), (1, 0)])


def dot32(left, right, dims):
    return lax.dot_general(left, right, (dims, ((), ())), preferred_element_type=jnp.float32)


def channel_gain_rows(channel_gain, channels):
    start = lax.axis_index("dp") * channels
    return lax.dynamic_slice_in_dim(channel_gain, start, channels, 0)[:, None]


def partner(index, distance, count):
    assert count & (count - 1) == 0
    return index ^ distance


def swap_columns(block, distance, keep=None):
    count = lax.axis_size("pipe")
    route = [(i, partner(i, distance, count)) for i in range(count)]
    route = [pair for pair in route if keep is None or keep(*pair)]
    return lax.ppermute(block, "pipe", route)


def choose(which, blocks):
    return lax.select_n(which, *blocks)


def after(block, *others):
    return lax.optimization_barrier((block,) + others)[0]


def exact_halves(values):
    high = lax.reduce_precision(values, 8, 7)
    return high.astype(jnp.bfloat16), (values - high).astype(jnp.bfloat16)


def centred_unit(values):
    values = values.astype(jnp.float32)
    center = values - jnp.mean(values, axis=-1, keepdims=True)
    inv_std = lax.rsqrt(jnp.mean(center * center, axis=-1, keepdims=True) + norm_eps)
    return center * inv_std, inv_std


def layer(llm_grad, slot_row, counts, saved_in, saved_pre, weights, channel_scale):
    sections = columns = lax.axis_size("pipe")
    ranks = lax.axis_size("dp")
    core = lax.axis_index("tensor")
    column = lax.axis_index("pipe")
    rank = lax.axis_index("dp")
    micro_count, row_count, model_width = llm_grad.shape
    hidden = saved_pre.shape[3]
    tokens = micro_count * row_count
    all_tokens = ranks * tokens
    channels = weights.shape[1]
    part = tokens // (2 * columns)
    piece = channels // columns
    starts, fresh, width = cuts(hidden, columns)
    gain_rows = channel_gain_rows(channel_scale[0], channels)
    ups = list(range(sections - 2, -1, -2))
    downs = list(range(sections - 1, -1, -2))
    own_fresh = lookup(fresh, column)
    is_fresh = lax.broadcasted_iota(jnp.int32, (1, width), 1) < own_fresh

    def mine(halves):
        return jnp.where(core == 0, halves[0], halves[1])

    def theirs(halves):
        return jnp.where(core == 0, halves[1], halves[0])

    def both_cores(block, axis):
        other = swap_cores(block)
        first = jnp.where(core == 0, block, other)
        second = jnp.where(core == 0, other, block)
        return jnp.stack([first, second], axis=axis)

    def hidden_piece(block, to):
        return lax.dynamic_slice_in_dim(block, lookup(starts, to), width, block.ndim - 1)

    def by_section(got):
        return [choose(partner(column, s, columns), got) for s in range(sections)]

    def scatter_hidden(block, ready=lambda piece: piece):
        pieces = [ready(hidden_piece(block, partner(column, d, columns))) for d in range(columns)]
        return [pieces[0]] + [swap_columns(pieces[d], d) for d in range(1, columns)]

    def token_halves(block):
        halves = block.reshape(ranks * columns, 2, part, channels)
        return halves[:, 0], halves[:, 1]

    def sum_to_rows(partial_sum, whole):
        halves = token_halves(partial_sum)
        given = theirs(halves).astype(jnp.bfloat16)
        pair = (mine(halves) + swap_cores(given).astype(jnp.float32)).astype(jnp.bfloat16)
        share = lax.dynamic_slice_in_dim(mine(token_halves(whole)), column * piece, piece, 2)
        got = exchange(jnp.concatenate([pair, share], axis=-1), ("dp", "pipe"))
        got = got.reshape(ranks, columns, part, channels + piece)
        summed = jnp.sum(got[..., :channels].astype(jnp.float32), axis=1)
        summed = summed.transpose(1, 0, 2).reshape(part, model_width)
        return summed, got[..., channels:].transpose(2, 0, 1, 3).reshape(part, model_width)

    def sum_over_ranks(partial_sum):
        sent = partial_sum.astype(jnp.bfloat16).reshape(ranks, tokens, -1)
        return jnp.sum(exchange(sent, "dp").astype(jnp.float32), axis=0)

    def all_ranks(block):
        sent = jnp.broadcast_to(block[None], (ranks,) + block.shape)
        return exchange(sent, "dp").reshape(all_tokens, -1)

    def all_ranks_aside(block):
        if ranks > aside_limit:
            sent = jnp.broadcast_to(block[None], (ranks,) + block.shape)
            return exchange(sent, "dp").reshape((all_tokens,) + block.shape[1:])
        got = [block]
        for distance in range(1, ranks):
            route = [(i, (i + distance) % ranks) for i in range(ranks)]
            got.append(lax.ppermute(block, "dp", route))
        return got

    def turned(block):
        by_rank = block.reshape(ranks, tokens, -1)
        if ranks > aside_limit:
            return block
        order = [
            lax.dynamic_index_in_dim(by_rank, (rank + ranks - d) % ranks, 0, keepdims=False)
            for d in range(ranks)
        ]
        return jnp.concatenate(order, axis=0)

    def to_channels(rows):
        return exchange(rows.transpose(1, 0, 2), "dp").reshape(all_tokens, -1)

    weight_got = scatter_hidden(
        weights[0], lambda block: (block.astype(jnp.float32) * gain_rows).astype(jnp.bfloat16)
    )
    top_rows = local_top(llm_grad, slot_row[:, 0], counts[0]).reshape(tokens, model_width)
    grad_all = to_channels(top_rows.reshape(tokens, ranks, channels))

    own_in = saved_in[0].reshape(tokens, model_width)
    own_unit, own_std = centred_unit(own_in)
    std_terms = jnp.stack(exact_halves(own_std), axis=-1)
    unit_sent = jnp.concatenate(
        [
            own_unit.astype(jnp.bfloat16).reshape(tokens, ranks, channels),
            jnp.broadcast_to(std_terms, (tokens, ranks, 2)),
        ],
        axis=-1,
    )
    unit_half = mine(to_channels(unit_sent).reshape(2, all_tokens // 2, channels + 2))
    grad_all = after(grad_all, unit_half)

    pre_flat = after(saved_pre[0].reshape(tokens, hidden), *weight_got)
    pre_parts = by_section(scatter_hidden(pre_flat))
    weight_parts = by_section(weight_got)
    unit_half = after(unit_half, *pre_parts)
    unit_got = [unit_half] + [
        swap_columns(unit_half, d, lambda a, b: a % 2 == 0) for d in range(1, columns)
    ]
    units = {s: both_cores(choose(partner(column, s, columns), unit_got), 0) for s in ups}
    units = {s: unit.reshape(all_tokens, channels + 2) for s, unit in units.items()}
    in_halves = own_in.reshape(columns, 2, part, model_width)
    in_halves = jnp.where(core == 0, in_halves[:, 0], in_halves[:, 1])
    in_got = [lax.dynamic_index_in_dim(in_halves, column, 0, keepdims=False)]
    for d in range(1, columns):
        to = partner(column, d, columns)
        sent = lax.dynamic_index_in_dim(in_halves, to, 0, keepdims=False)
        in_got.append(swap_columns(sent, d, lambda a, b: a == 0))
    last_in = choose(column, in_got)

    def hidden_chain(down, up, grad):
        partial_hidden = dot32(grad, weight_parts[down], ((1,), (0,)))
        slope = gelu_parts(pre_parts[up].astype(jnp.float32))[1]
        slope = lax.optimization_barrier(slope)
        return (sum_over_ranks(partial_hidden) * slope).astype(jnp.bfloat16)

    def input_grad(up, act_grad):
        fresh_weight = jnp.where(is_fresh, weight_parts[up], jnp.zeros_like(weight_parts[up]))
        return dot32(act_grad, fresh_weight, ((1,), (1,)))

    def norm_back(incoming, back, unit, inv_std, mean_back, mean_both):
        back = inv_std * (back - mean_back - unit * mean_both)
        return (incoming.astype(jnp.float32) + back).astype(jnp.bfloat16)

    def activated(s):
        return gelu_parts(pre_parts[s].astype(jnp.float32))[0].astype(jnp.bfloat16)

    sides = [None] * sections
    grads = {downs[0]: grad_all}
    for up, down in zip(ups[:-1], downs):
        act_grad = all_ranks(hidden_chain(down, up, grad_all))
        sides[up] = (units[up][:, :channels], act_grad)
        back = input_grad(up, act_grad)
        unit = units[up][:, :channels].astype(jnp.float32)
        sums = jnp.stack([jnp.sum(back, axis=1), jnp.sum(back * unit, axis=1)])
        sums = sums.reshape(2 * all_tokens // lanes, lanes)
        devices = ranks * columns * 2
        sums = exchange(
            jnp.broadcast_to(sums[None], (devices,) + sums.shape), ("dp", "pipe", "tensor")
        )
        sums = (jnp.sum(sums, axis=0) / model_width).reshape(2, all_tokens)
        halves = back.reshape(2, all_tokens // 2, channels)
        pair = mine(halves) + swap_cores(theirs(halves).astype(jnp.bfloat16)).astype(jnp.float32)
        pair = pair.astype(jnp.bfloat16)
        summed = pair.astype(jnp.float32)
        for d in range(1, columns):
            summed = summed + swap_columns(pair, d).astype(jnp.float32)
        own_unit_half = mine(units[up].reshape(2, all_tokens // 2, channels + 2)).astype(jnp.float32)
        own_sums = mine(sums.reshape(2, 2, all_tokens // 2).transpose(1, 0, 2))
        new_half = norm_back(
            mine(grad_all.reshape(2, all_tokens // 2, channels)),
            summed,
            own_unit_half[:, :channels],
            own_unit_half[:, channels : channels + 1] + own_unit_half[:, channels + 1 :],
            own_sums[0][:, None],
            own_sums[1][:, None],
        )
        grad_all = both_cores(new_half, 0).reshape(all_tokens, channels)
        grads[down - 2] = grad_all
    down, up = downs[-1], ups[-1]
    activated_own = jnp.concatenate([activated(s) for s in downs], axis=1)
    activated_all = all_ranks_aside(activated_own)
    act_grad = all_ranks(hidden_chain(down, up, grad_all))
    sides[up] = (units[up][:, :channels], act_grad)
    if ranks <= aside_limit:
        activated_all = jnp.concatenate(activated_all, axis=0)
        activated_all = lax.optimization_barrier(activated_all)
    for i, s in enumerate(downs):
        sides[s] = (turned(grads[s]), activated_all[:, i * width : (i + 1) * width])
    weight_grads = [
        lax.optimization_barrier(dot32(*pair, ((0,), (0,))).astype(jnp.bfloat16)) for pair in sides
    ]

    back, own_rows = sum_to_rows(input_grad(up, act_grad), grad_all)
    unit, inv_std = centred_unit(last_in)
    last_rows = norm_back(
        own_rows,
        back,
        unit,
        inv_std,
        jnp.mean(back, axis=-1, keepdims=True),
        jnp.mean(back * unit, axis=-1, keepdims=True),
    )

    def placed(out, block, source):
        block = (block.astype(jnp.float32) * gain_rows).astype(jnp.bfloat16)
        return lax.dynamic_update_slice_in_dim(out, block, lookup(starts, source), 1)

    weight_out = jnp.zeros((channels, hidden), jnp.bfloat16)
    weight_out = placed(weight_out, choose(column, weight_grads), column)
    last_grad = weight_grads[0]
    arrived = {}
    for d in range(1, columns):
        early = after(choose(partner(column, d, columns), [weight_grads[1]] + weight_grads[1:]))
        arrived[d] = swap_columns(early, d, lambda a, b: b > 0)
    if columns == 4:
        cut = channels // 32 * 16
        relayed = swap_columns(last_grad[cut:], 2, lambda a, b: a == 3)
    late = {}
    for d in (2, 3, 1) if columns == 4 else range(1, columns):
        if columns == 4 and d == 3:
            direct = swap_columns(last_grad[:cut], 3, lambda a, b: b == 0)
            relayed = swap_columns(relayed, 1, lambda a, b: b == 0)
            late[d] = jnp.concatenate([direct, relayed], axis=0)
        else:
            late[d] = swap_columns(last_grad, d, lambda a, b: b == 0)
    for d in range(1, columns):
        block = jnp.where(column == 0, late[d], arrived[d])
        weight_out = placed(weight_out, block, partner(column, d, columns))

    rows_of = [last_rows] + [own_rows] * (sections - 1)
    rows_got = [choose(column, rows_of)]
    for d in range(1, columns):
        sent = choose(partner(column, d, columns), rows_of)
        rows_got.append(swap_columns(sent, d, lambda a, b: b < sections - 1))
    rows_got = jnp.stack([choose(partner(column, m, columns), rows_got) for m in range(columns)])
    rows_got = both_cores(rows_got, 1).reshape(tokens, model_width)
    section_out = jnp.where(column == sections - 1, top_rows, rows_got)
    return (weight_out[None], section_out.reshape(1, micro_count, row_count, model_width))


def solution(mesh):
    in_specs = (
        P(None, "dp", None),
        P(None, "dp", None),
        P("dp", None),
        P("pipe", None, "dp", None),
        P("pipe", None, "dp", "tensor"),
        P("pipe", "dp", "tensor"),
        P("pipe", None),
    )
    out_specs = (P("pipe", "dp", "tensor"), P("pipe", None, "dp", None))
    return jax.shard_map(layer, mesh=mesh, in_specs=in_specs, out_specs=out_specs, check_vma=False)
```

```python
import jax
import jax.numpy as jnp
from jax import lax
from jax.sharding import PartitionSpec as P

norm_eps = 1e-06
root_half = 0.7071067811865476
inv_root_two_pi = 0.3989422804014327
lanes = 128
aside_limit = 8


def gelu_parts(pre_act):
    normal_cdf = 0.5 * (1.0 + jax.scipy.special.erf(pre_act * root_half))
    density = jnp.exp(-0.5 * pre_act * pre_act) * inv_root_two_pi
    return (pre_act * normal_cdf, normal_cdf + pre_act * density)


def local_top(llm_grad, slot_row, counts):
    row_count = llm_grad.shape[1]
    slot_ids = jnp.arange(row_count, dtype=jnp.int32)
    kept_mask = slot_ids[None, :] < counts[:, None]
    source = jnp.where(kept_mask[..., None], llm_grad, jnp.zeros_like(llm_grad))
    onehot = (slot_row[:, :, None] == slot_ids[None, None, :]).astype(jnp.bfloat16)
    placed = jnp.einsum("mjr,mjd->mrd", onehot, source, preferred_element_type=jnp.float32)
    return placed.astype(jnp.bfloat16)


def cuts(hidden, parts):
    unit = lanes if hidden % lanes == 0 else 1
    tiles = hidden // unit
    bounds = [tiles * i // parts * unit for i in range(parts + 1)]
    width = max(b - a for a, b in zip(bounds, bounds[1:]))
    starts = [min(a, hidden - width) for a in bounds[:-1]]
    fresh = [b - a for a, b in zip(starts, starts[1:] + [hidden])]
    return starts, fresh, width


def lookup(values, index):
    found = jnp.int32(values[-1])
    for i, value in enumerate(values[:-1]):
        found = jnp.where(index == i, jnp.int32(value), found)
    return found


def exchange(blocks, axes):
    return lax.all_to_all(blocks, axes, 0, 0, tiled=True)


def swap_cores(block):
    return lax.ppermute(block, "tensor", [(0, 1), (1, 0)])


def dot32(left, right, dims):
    return lax.dot_general(left, right, (dims, ((), ())), preferred_element_type=jnp.float32)


def channel_gain_rows(channel_gain, channels):
    start = lax.axis_index("dp") * channels
    return lax.dynamic_slice_in_dim(channel_gain, start, channels, 0)[:, None]


def partner(index, distance, count):
    assert count & (count - 1) == 0
    return index ^ distance


def swap_columns(block, distance, keep=None):
    count = lax.axis_size("pipe")
    route = [(i, partner(i, distance, count)) for i in range(count)]
    route = [pair for pair in route if keep is None or keep(*pair)]
    return lax.ppermute(block, "pipe", route)


def choose(which, blocks):
    return lax.select_n(which, *blocks)


def after(block, *others):
    return lax.optimization_barrier((block,) + others)[0]


def exact_halves(values):
    high = lax.reduce_precision(values, 8, 7)
    return high.astype(jnp.bfloat16), (values - high).astype(jnp.bfloat16)


def centred_unit(values):
    values = values.astype(jnp.float32)
    center = values - jnp.mean(values, axis=-1, keepdims=True)
    inv_std = lax.rsqrt(jnp.mean(center * center, axis=-1, keepdims=True) + norm_eps)
    return center * inv_std, inv_std


def layer(llm_grad, slot_row, counts, saved_in, saved_pre, weights, channel_scale):
    sections = columns = lax.axis_size("pipe")
    ranks = lax.axis_size("dp")
    core = lax.axis_index("tensor")
    column = lax.axis_index("pipe")
    rank = lax.axis_index("dp")
    micro_count, row_count, model_width = llm_grad.shape
    hidden = saved_pre.shape[3]
    tokens = micro_count * row_count
    all_tokens = ranks * tokens
    channels = weights.shape[1]
    part = tokens // (2 * columns)
    piece = channels // columns
    starts, fresh, width = cuts(hidden, columns)
    gain_rows = channel_gain_rows(channel_scale[0], channels)
    ups = list(range(sections - 2, -1, -2))
    downs = list(range(sections - 1, -1, -2))
    own_fresh = lookup(fresh, column)
    is_fresh = lax.broadcasted_iota(jnp.int32, (1, width), 1) < own_fresh

    def mine(halves):
        return jnp.where(core == 0, halves[0], halves[1])

    def theirs(halves):
        return jnp.where(core == 0, halves[1], halves[0])

    def both_cores(block, axis):
        other = swap_cores(block)
        first = jnp.where(core == 0, block, other)
        second = jnp.where(core == 0, other, block)
        return jnp.stack([first, second], axis=axis)

    def hidden_piece(block, to):
        return lax.dynamic_slice_in_dim(block, lookup(starts, to), width, block.ndim - 1)

    def by_section(got):
        return [choose(partner(column, s, columns), got) for s in range(sections)]

    def scatter_hidden(block, ready=lambda piece: piece):
        pieces = [ready(hidden_piece(block, partner(column, d, columns))) for d in range(columns)]
        return [pieces[0]] + [swap_columns(pieces[d], d) for d in range(1, columns)]

    def token_halves(block):
        halves = block.reshape(ranks * columns, 2, part, channels)
        return halves[:, 0], halves[:, 1]

    def to_channels_aside(rows, finish):
        if ranks > aside_limit:
            blocks = [finish(rows[:, j]) for j in range(ranks)]
            return exchange(jnp.stack(blocks), "dp")
        got = []
        for distance in range(ranks):
            to = (rank + distance) % ranks
            block = finish(lax.dynamic_index_in_dim(rows, to, 1, keepdims=False))
            if distance > 0:
                route = [(i, (i + distance) % ranks) for i in range(ranks)]
                block = lax.ppermute(block, "dp", route)
            got.append(block)
        by_rank = [choose((rank + ranks - j) % ranks, got) for j in range(ranks)]
        return jnp.stack(by_rank)

    def sum_to_rows(partial_sum, *wholes):
        halves = token_halves(partial_sum)
        given = theirs(halves).astype(jnp.bfloat16)
        pair = (mine(halves) + swap_cores(given).astype(jnp.float32)).astype(jnp.bfloat16)
        shares = [
            lax.dynamic_slice_in_dim(mine(token_halves(whole)), column * piece, piece, 2)
            for whole in wholes
        ]
        got = exchange(jnp.concatenate([pair] + shares, axis=-1), ("dp", "pipe"))
        got = got.reshape(ranks, columns, part, channels + len(wholes) * piece)
        summed = jnp.sum(got[..., :channels].astype(jnp.float32), axis=1)
        rows = [summed.transpose(1, 0, 2).reshape(part, model_width)]
        for i in range(len(wholes)):
            share = got[..., channels + i * piece : channels + (i + 1) * piece]
            rows.append(share.transpose(2, 0, 1, 3).reshape(part, model_width))
        return rows

    def sum_over_ranks(partial_sum):
        sent = partial_sum.astype(jnp.bfloat16).reshape(ranks, tokens, -1)
        return jnp.sum(exchange(sent, "dp").astype(jnp.float32), axis=0)

    def all_ranks(block):
        sent = jnp.broadcast_to(block[None], (ranks,) + block.shape)
        return exchange(sent, "dp").reshape(all_tokens, -1)

    def all_ranks_aside(block):
        if ranks > aside_limit:
            sent = jnp.broadcast_to(block[None], (ranks,) + block.shape)
            return exchange(sent, "dp").reshape((all_tokens,) + block.shape[1:])
        got = [block]
        for distance in range(1, ranks):
            route = [(i, (i + distance) % ranks) for i in range(ranks)]
            got.append(lax.ppermute(block, "dp", route))
        return got

    def turned(block):
        by_rank = block.reshape(ranks, tokens, -1)
        if ranks > aside_limit:
            return block
        order = [
            lax.dynamic_index_in_dim(by_rank, (rank + ranks - d) % ranks, 0, keepdims=False)
            for d in range(ranks)
        ]
        return jnp.concatenate(order, axis=0)

    def core_half(rows):
        return mine(rows.reshape(2, tokens // 2, ranks, channels))

    def both_halves(block):
        return both_cores(block, 1).reshape(all_tokens, -1)

    def to_channels(rows):
        return exchange(rows.transpose(1, 0, 2), "dp")

    top = sections - 1
    cut = channels // 32 * 16

    def weight_piece(distance):
        block = hidden_piece(weights[0], partner(column, distance, columns))
        return (block.astype(jnp.float32) * gain_rows).astype(jnp.bfloat16)

    weight_pieces = [weight_piece(d) for d in range(columns)]
    top_weight = [weight_pieces[0]] * columns
    if columns == 4:
        from_top = lambda a, b: a == top
        over_2 = swap_columns(weight_pieces[3][:cut], 1, from_top)
        over_1 = swap_columns(weight_pieces[3][cut:], 2, from_top)
        top_weight[2] = swap_columns(weight_pieces[1], 1, from_top)
        top_weight[1] = swap_columns(weight_pieces[2], 2, from_top)
        over_2 = swap_columns(over_2, 2, lambda a, b: b == 0)
        over_1 = swap_columns(over_1, 1, lambda a, b: b == 0)
        top_weight[0] = jnp.concatenate([over_2, over_1], axis=0)
    else:
        for d in range(1, columns):
            top_weight[partner(top, d, columns)] = swap_columns(
                weight_pieces[d], d, lambda a, b: a == top
            )
    top_weight = choose(column, top_weight)
    top_rows = local_top(llm_grad, slot_row[:, 0], counts[0]).reshape(tokens, model_width)
    grad_all = both_halves(to_channels(core_half(top_rows)))

    own_in = saved_in[0].reshape(tokens, model_width)
    own_unit, own_std = centred_unit(own_in)
    std_terms = [mine(term.reshape(2, tokens // 2, 1)) for term in exact_halves(own_std)]
    wide = -(-(channels + 2) // lanes) * lanes
    lane = lax.broadcasted_iota(jnp.int32, (tokens // 2, wide), 1)

    def with_std(block):
        block = jnp.pad(block, [(0, 0), (0, wide - channels)])
        block = jnp.where(lane == channels, std_terms[0], block)
        return jnp.where(lane == channels + 1, std_terms[1], block)

    unit_half = to_channels_aside(core_half(own_unit.astype(jnp.bfloat16)), with_std)

    pre_parts = by_section(scatter_hidden(saved_pre[0].reshape(tokens, hidden)))
    weight_got = [weight_pieces[0]] + [
        swap_columns(weight_pieces[d], d, lambda a, b: a != top)
        for d in range(1, columns)
    ]
    weight_parts = by_section(weight_got)[:top]
    weight_parts = by_section(weight_got)[: top - 1] + weight_parts[top - 1 :]
    weight_parts = [lax.optimization_barrier(part) for part in weight_parts[: top - 1]] + [
        weight_parts[top - 1],
        top_weight,
    ]
    unit_got = [unit_half] + [
        swap_columns(unit_half, d, lambda a, b: a % 2 == 0) for d in range(1, columns)
    ]
    units = {s: both_halves(choose(partner(column, s, columns), unit_got)) for s in ups}
    stds = {
        s: jnp.sum(block[:, channels : channels + 2].astype(jnp.float32), axis=1, keepdims=True)
        for s, block in units.items()
    }
    units = {s: block[:, :channels] for s, block in units.items()}

    def hidden_chain(down, up, grad):
        partial_hidden = dot32(grad, weight_parts[down], ((1,), (0,)))
        slope = gelu_parts(pre_parts[up].astype(jnp.float32))[1]
        slope = lax.optimization_barrier(slope)
        return (sum_over_ranks(partial_hidden) * slope).astype(jnp.bfloat16)

    def input_grad(up, act_grad):
        fresh_weight = jnp.where(is_fresh, weight_parts[up], jnp.zeros_like(weight_parts[up]))
        return dot32(act_grad, fresh_weight, ((1,), (1,)))

    def norm_back(incoming, back, unit, inv_std, mean_back, mean_both):
        back = inv_std * (back - mean_back - unit * mean_both)
        return (incoming.astype(jnp.float32) + back).astype(jnp.bfloat16)

    def activated(s):
        return gelu_parts(pre_parts[s].astype(jnp.float32))[0].astype(jnp.bfloat16)

    sides = [None] * sections
    grads = {downs[0]: grad_all}
    for up, down in zip(ups[:-1], downs):
        act_grad = all_ranks(hidden_chain(down, up, grad_all))
        sides[up] = (units[up], act_grad)
        back = input_grad(up, act_grad)
        unit = units[up].astype(jnp.float32)
        sums = jnp.stack([jnp.sum(back, axis=1), jnp.sum(back * unit, axis=1)])
        sums = sums.reshape(2 * all_tokens // lanes, lanes)
        devices = ranks * columns * 2
        sums = exchange(
            jnp.broadcast_to(sums[None], (devices,) + sums.shape), ("dp", "pipe", "tensor")
        )
        sums = jnp.sum(sums, axis=0).reshape(2, all_tokens)
        halves = back.reshape(2, all_tokens // 2, channels)
        pair = mine(halves) + swap_cores(theirs(halves).astype(jnp.bfloat16)).astype(jnp.float32)
        pair = pair.astype(jnp.bfloat16)
        summed = pair.astype(jnp.float32)
        for d in range(1, columns):
            summed = summed + swap_columns(pair, d).astype(jnp.float32)
        own_sums = mine(sums.reshape(2, 2, all_tokens // 2).transpose(1, 0, 2))[:, :, None]
        new_half = norm_back(
            mine(grad_all.reshape(2, all_tokens // 2, channels)),
            summed,
            mine(units[up].reshape(2, all_tokens // 2, channels)).astype(jnp.float32),
            mine(stds[up].reshape(2, all_tokens // 2, 1)),
            own_sums[0] / model_width,
            own_sums[1] / model_width,
        )
        grad_all = both_cores(new_half, 0).reshape(all_tokens, channels)
        grads[down - 2] = grad_all
    down, up = downs[-1], ups[-1]
    activated_own = jnp.concatenate([activated(s) for s in downs], axis=1)
    activated_all = all_ranks_aside(lax.optimization_barrier(activated_own))
    act_grad = all_ranks(hidden_chain(down, up, grad_all))
    sides[up] = (units[up], act_grad)
    if ranks <= aside_limit:
        activated_all = jnp.concatenate(activated_all, axis=0)
        activated_all = lax.optimization_barrier(activated_all)
    for i, s in enumerate(downs):
        sides[s] = (turned(grads[s]), activated_all[:, i * width : (i + 1) * width])
    weight_grads = [
        lax.optimization_barrier(dot32(*pair, ((0,), (0,))).astype(jnp.bfloat16)) for pair in sides
    ]

    back, own_rows, unit = sum_to_rows(input_grad(up, act_grad), grad_all, units[up])
    unit = unit.astype(jnp.float32)
    inv_std = lax.dynamic_slice_in_dim(
        stds[up], rank * tokens + (2 * column + core) * part, part, 0
    )
    last_rows = norm_back(
        own_rows,
        back,
        unit,
        inv_std,
        jnp.mean(back, axis=-1, keepdims=True),
        jnp.mean(back * unit, axis=-1, keepdims=True),
    )

    def placed(out, block, source):
        block = (block.astype(jnp.float32) * gain_rows).astype(jnp.bfloat16)
        return lax.dynamic_update_slice_in_dim(out, block, lookup(starts, source), 1)

    weight_out = jnp.zeros((channels, hidden), jnp.bfloat16)
    weight_out = placed(weight_out, choose(column, weight_grads), column)
    last_grad = weight_grads[0]
    arrived = {}
    for d in range(1, columns):
        early = after(choose(partner(column, d, columns), [weight_grads[1]] + weight_grads[1:]))
        arrived[d] = swap_columns(early, d, lambda a, b: b > 0)
    if columns == 4:
        relayed = swap_columns(last_grad[cut:], 2, lambda a, b: a == 3)
    late = {}
    for d in (2, 3, 1) if columns == 4 else range(1, columns):
        if columns == 4 and d == 3:
            direct = swap_columns(last_grad[:cut], 3, lambda a, b: b == 0)
            relayed = swap_columns(relayed, 1, lambda a, b: b == 0)
            late[d] = jnp.concatenate([direct, relayed], axis=0)
        else:
            late[d] = swap_columns(last_grad, d, lambda a, b: b == 0)
    for d in range(1, columns):
        block = jnp.where(column == 0, late[d], arrived[d])
        weight_out = placed(weight_out, block, partner(column, d, columns))

    rows_of = [last_rows] + [own_rows] * (sections - 1)
    rows_got = exchange(jnp.stack(rows_of), "pipe")
    rows_got = both_cores(rows_got, 1).reshape(tokens, model_width)
    section_out = jnp.where(column == sections - 1, top_rows, rows_got)
    return (weight_out[None], section_out.reshape(1, micro_count, row_count, model_width))


def solution(mesh):
    in_specs = (
        P(None, "dp", None),
        P(None, "dp", None),
        P("dp", None),
        P("pipe", None, "dp", None),
        P("pipe", None, "dp", "tensor"),
        P("pipe", "dp", "tensor"),
        P("pipe", None),
    )
    out_specs = (P("pipe", "dp", "tensor"), P("pipe", None, "dp", None))
    return jax.shard_map(layer, mesh=mesh, in_specs=in_specs, out_specs=out_specs, check_vma=False)
```
